32 devices in a mesh: ctx: 8 (over z, y), head: 2 (over x), section: 2 (over core).
Axes of the slice: x: 2, y: 2, z: 4, core: 2. Of those that a mesh axis runs over, the one named last changes fastest.
Arguments:
- delta_query: bfloat16 [2, 1024, 2048], P('section', 'ctx', 'head'), may hold values from -6 to 6
- delta_key: bfloat16 [2, 1024, 2048], P('section', 'ctx', 'head'), may hold values from -6 to 6
- delta_value: bfloat16 [2, 1024, 2048], P('section', 'ctx', 'head'), may hold values from -6 to 6
- beta_logit: float32 [2, 1024, 16], P('section', 'ctx', 'head'), may hold values from -6 to 6
- decay_input: float32 [2, 1024, 16], P('section', 'ctx', 'head'), may hold values from -4 to 9216
- decay_log: float32 [16], P('head'), may hold values from -14 to -2
- norm_gain: float32 [128], replicated, may hold values from 0.25 to 1.75
- output_gate: bfloat16 [2, 1024, 2048], P('section', 'ctx', 'head'), may hold values from -6 to 6
- delta_cotangent: bfloat16 [2, 1024, 2048], P('section', 'ctx', 'head'), may hold values from -12 to 12
- attn_query: bfloat16 [2, 1024, 4096], P('section', 'ctx', 'head'), may hold values from -5 to 5
- attn_key: bfloat16 [2, 1024, 512], P('section', 'ctx', 'head'), may hold values from -5 to 5
- attn_value: bfloat16 [2, 1024, 512], P('section', 'ctx', 'head'), may hold values from -6 to 6
- attn_gate: bfloat16 [2, 1024, 4096], P('section', 'ctx', 'head'), may hold values from -6 to 6
- attn_cotangent: bfloat16 [2, 1024, 4096], P('section', 'ctx', 'head'), may hold values from -6 to 6
Outputs:
- delta_output: bfloat16 [2, 1024, 2048], P('section', 'ctx', 'head')
- grad_delta_query: bfloat16 [2, 1024, 2048], P('section', 'ctx', 'head')
- grad_delta_key: bfloat16 [2, 1024, 2048], P('section', 'ctx', 'head')
- grad_delta_value: bfloat16 [2, 1024, 2048], P('section', 'ctx', 'head')
- grad_beta_logit: float32 [2, 1024, 16], P('section', 'ctx', 'head')
- grad_decay_input: float32 [2, 1024, 16], P('section', 'ctx', 'head')
- grad_decay_log: float32 [16], P('head')
- grad_norm_gain: float32 [128], replicated
- grad_output_gate: bfloat16 [2, 1024, 2048], P('section', 'ctx', 'head')
- attn_output: bfloat16 [2, 1024, 4096], P('section', 'ctx', 'head')
- grad_attn_query: bfloat16 [2, 1024, 4096], P('section', 'ctx', 'head')
- grad_attn_key: bfloat16 [2, 1024, 512], P('section', 'ctx', 'head')
- grad_attn_value: bfloat16 [2, 1024, 512], P('section', 'ctx', 'head')
- grad_attn_gate: bfloat16 [2, 1024, 4096], P('section', 'ctx', 'head')
The draws below stay inside these ranges and needn't reach their ends.
All inputs are finite; a program needn't handle non-finite values.
Results may differ from the reference program's by a relative error of at most 0.02.
Values may be sent and summed in bfloat16 or wider, within the bound.
No kernel may reach another device: no remote copies, remote signals or barrier semaphores. Data moves between devices by JAX's collectives and lax.ppermute only.
A program may use at most 256 MiB of HBM per device.

```python
import math
import jax
import jax.numpy as jnp
from jax import lax

DK = 128
DHEADS = 16
BLOCK_LEN = 64
AHEADS = 16
KVHEADS = 2
AD = 256
TOK_DEV = 128
LENGTH = 1024
SEQS = 2


def decay_pair(key):
    rate_key = jax.random.fold_in(key, 11)
    logs = jax.random.uniform(rate_key, (DHEADS,), jnp.float32, math.log(0.08 / LENGTH), math.log(0.06))
    stochastic_perturbation = 0.7 * jnp.clip(jax.random.normal(jax.random.fold_in(key, 12), (SEQS, LENGTH, DHEADS), jnp.float32), -4.0, 4.0)
    speed_amounts = jnp.exp(logs)
    beginning_shifts = jax.random.uniform(jax.random.fold_in(key, 13), (SEQS, LENGTH // TOK_DEV, DHEADS), jnp.float32, -1.0, 1.0)
    beginning_shifts = jnp.repeat(beginning_shifts, TOK_DEV, axis=1)
    spots = jax.random.randint(jax.random.fold_in(key, 14), (SEQS, 4), 0, LENGTH, dtype=jnp.int32)
    location_sequence = jnp.arange(LENGTH, dtype=jnp.int32)[None, :, None] == spots[:, None, :]
    token_clusters = jnp.any(location_sequence, axis=-1)
    portion_fractions = jax.random.uniform(jax.random.fold_in(key, 15), (SEQS, LENGTH, DHEADS), jnp.float32, 0.25, 0.65)
    opening_multipliers = jnp.where(token_clusters[:, :, None], portion_fractions / speed_amounts[None, None, :], stochastic_perturbation + beginning_shifts)
    return (logs, opening_multipliers)


def draw_decay_log(key, part):
    return decay_pair(key)[0].astype(jnp.float32)


def draw_decay_input(key, part):
    return decay_pair(key)[1].astype(jnp.float32)


def draw_delta_cotangent(key, part):
    positions = jnp.arange(LENGTH, dtype=jnp.float32)[None, :, None] / LENGTH
    drawn = jnp.clip(jax.random.normal(key, (SEQS, LENGTH, DHEADS * DK), jnp.float32), -5.0, 5.0) * (0.5 + 1.5 * positions)
    return drawn.astype(jnp.bfloat16)


def drawn_pair(key):
    query_key = jax.random.fold_in(key, 21)
    keys_key = jax.random.fold_in(key, 22)
    queries = jnp.clip(jax.random.normal(query_key, (SEQS, LENGTH, AHEADS * AD), jnp.float32), -4.5, 4.5)
    keys_drawn = jnp.clip(jax.random.normal(keys_key, (SEQS, LENGTH, KVHEADS * AD), jnp.float32), -4.5, 4.5)
    return (queries, keys_drawn)


def draw_attn_query(key, part):
    return drawn_pair(key)[0].astype(jnp.bfloat16)


def draw_attn_key(key, part):
    return drawn_pair(key)[1].astype(jnp.bfloat16)


def level_of(own_key, extent, split, smallest, largest):
    def one(dim, parts):
        steps = jax.random.uniform(jax.random.fold_in(jax.random.fold_in(own_key, 6), dim), (parts,), jnp.float32, smallest / len(split), largest / len(split))
        return jnp.repeat(jnp.exp(steps), extent[dim] // parts).reshape((-1,) + (1,) * (len(extent) - dim - 1))

    factor_of = one(*split[0])
    for cut in split[1:]:
        factor_of = factor_of * one(*cut)
    return factor_of


def gaussian(key, dims, scale, most, split=(), kind=jnp.bfloat16):
    values = jax.random.normal(key, dims, jnp.float32) * scale
    if len(split) > 0:
        values = level_of(key, dims, split, -0.22, 0.18) * values
    return jnp.clip(values, min=-most, max=most).astype(kind)


def setup_inputs(seed: int = 0) -> dict:
    streams_of = jax.random.split(jax.random.key(seed), 15)
    return {
        "delta_query": gaussian(streams_of[0], (SEQS, LENGTH, DHEADS * DK), 1.0, 6.0, ((0, 2), (1, 8), (2, 2))),
        "delta_key": gaussian(streams_of[1], (SEQS, LENGTH, DHEADS * DK), 1.0, 6.0, ((0, 2), (1, 8), (2, 2))),
        "delta_value": gaussian(streams_of[2], (SEQS, LENGTH, DHEADS * DK), 1.0, 6.0, ((0, 2), (1, 8), (2, 2))),
        "beta_logit": gaussian(streams_of[3], (SEQS, LENGTH, DHEADS), 1.5, 6.0, ((0, 2), (1, 8), (2, 2)), jnp.float32),
        "decay_input": draw_decay_input(jax.random.fold_in(streams_of[14], 71), 0),
        "decay_log": draw_decay_log(jax.random.fold_in(streams_of[14], 71), 0),
        "norm_gain": jnp.clip(1.0 + 0.15 * jax.random.normal(streams_of[6], (DK,), jnp.float32), 0.25, 1.75),
        "output_gate": gaussian(streams_of[7], (SEQS, LENGTH, DHEADS * DK), 1.0, 6.0, ((0, 2), (1, 8), (2, 2))),
        "delta_cotangent": draw_delta_cotangent(jax.random.fold_in(streams_of[14], 71), 0),
        "attn_query": draw_attn_query(jax.random.fold_in(streams_of[14], 71), 0),
        "attn_key": draw_attn_key(jax.random.fold_in(streams_of[14], 71), 0),
        "attn_value": gaussian(streams_of[11], (SEQS, LENGTH, KVHEADS * AD), 1.0, 6.0, ((0, 2), (1, 8), (2, 2))),
        "attn_gate": gaussian(streams_of[12], (SEQS, LENGTH, AHEADS * AD), 1.5, 6.0, ((0, 2), (1, 8), (2, 2))),
        "attn_cotangent": gaussian(streams_of[13], (SEQS, LENGTH, AHEADS * AD), 1.0, 6.0, ((0, 2), (1, 8), (2, 2))),
    }


HIGHEST = lax.Precision.HIGHEST
NEG_FILL = -1e+30

def unit_rows(values):
    return values * lax.rsqrt(lax.optimization_barrier(jnp.sum(values * values, axis=-1, keepdims=True)) + 1e-06)

def decay_inverse(lower_part):
    block_rows = lower_part.shape[-1]
    identity = jnp.eye(block_rows, dtype=jnp.float32)
    result = identity - lower_part
    powered = lower_part
    for doubling in range(block_rows.bit_length() - 2):
        powered = jnp.einsum('hij,hjk->hik', powered, powered, precision=HIGHEST)
        result = jnp.einsum('hij,hjk->hik', result, identity + powered, precision=HIGHEST)
    return result

def split_rows(array, block_rows):
    shaped = array.reshape((array.shape[0] // block_rows, block_rows) + array.shape[1:])
    return jnp.swapaxes(shaped, 1, 2)

def delta_inputs(queries, keys_in, beta_in, decay_in, decay_rates):
    scaling = queries.shape[-1] ** (-0.5)
    unit_queries = unit_rows(queries) * scaling
    unit_keys = unit_rows(keys_in)
    beta_values = jax.nn.sigmoid(beta_in)
    decays = -jnp.exp(decay_rates)[None, :] * jax.nn.softplus(decay_in)
    return (unit_queries, unit_keys, beta_values, decays)

def block_terms(keys_in, values, beta_values, decays):
    block_rows = decays.shape[1]
    cumulative = jnp.cumsum(decays, axis=1)
    row_ids = lax.broadcasted_iota(jnp.int32, (block_rows, block_rows), 0)
    col_ids = lax.broadcasted_iota(jnp.int32, (block_rows, block_rows), 1)
    strict = row_ids > col_ids
    within = row_ids >= col_ids
    spread = cumulative[:, :, None] - cumulative[:, None, :]
    fading = jnp.exp(jnp.where(within, spread, 0.0))
    products = jnp.einsum('hcd,hed->hce', keys_in, keys_in, precision=HIGHEST)
    lower_part = jnp.where(strict, beta_values[:, :, None] * fading * products, 0.0)
    solved = decay_inverse(lower_part)
    value_part = jnp.einsum('hce,hev->hcv', solved, beta_values[:, :, None] * values, precision=HIGHEST)
    key_part = jnp.einsum('hce,hed->hcd', solved, (beta_values * jnp.exp(cumulative))[:, :, None] * keys_in, precision=HIGHEST)
    tail_decay = jnp.exp(cumulative[:, -1:] - cumulative)
    return (cumulative, fading, within, value_part, key_part, tail_decay)

def block_output(state, terms, queries, keys_in):
    cumulative, fading, within, value_part, key_part, tail_decay = terms
    update = value_part - jnp.einsum('hcd,hvd->hcv', key_part, state, precision=HIGHEST)
    scores = jnp.where(within, jnp.einsum('hcd,hed->hce', queries, keys_in, precision=HIGHEST) * fading, 0.0)
    carried = jnp.exp(cumulative)[:, :, None] * jnp.einsum('hcd,hvd->hcv', queries, state, precision=HIGHEST)
    output = carried + jnp.einsum('hce,hev->hcv', scores, update, precision=HIGHEST)
    weighted = tail_decay[:, :, None] * keys_in
    state_next = jnp.exp(cumulative[:, -1])[:, None, None] * state + jnp.einsum('hcv,hcd->hvd', update, weighted, precision=HIGHEST)
    return (output, state_next)

def delta_layer(state, queries, keys_in, values, beta_in, decay_in, decay_rates, gain_in, gate_values, block_rows):
    unit_queries, unit_keys, beta_values, decays = delta_inputs(queries, keys_in, beta_in, decay_in, decay_rates)
    tokens, heads, head_size = queries.shape

    def advance(carried, pieces):
        block_queries, block_keys, block_values, block_betas, block_decays = pieces
        terms = block_terms(block_keys, block_values, block_betas, block_decays)
        output, carried_next = block_output(carried, terms, block_queries, block_keys)
        return (carried_next, output)
    pieces = (split_rows(unit_queries, block_rows), split_rows(unit_keys, block_rows), split_rows(values, block_rows), split_rows(beta_values, block_rows), split_rows(decays, block_rows))
    state_end, outputs = lax.scan(advance, state, pieces)
    mixture = jnp.swapaxes(outputs, 1, 2).reshape(tokens, heads, head_size)
    normed = mixture * lax.rsqrt(lax.optimization_barrier(jnp.mean(mixture * mixture, axis=-1, keepdims=True)) + 1e-06)
    return (normed * gain_in * jax.nn.silu(gate_values), state_end)

def block_scores(queries, key_block, query_start, key_start):
    scores = jnp.einsum('ikgd,jkd->kgij', queries.astype(jnp.float32), key_block.astype(jnp.float32)) * queries.shape[-1] ** (-0.5)
    rows_at = query_start + lax.broadcasted_iota(jnp.int32, (queries.shape[0], key_block.shape[0]), 0)
    cols_at = key_start + lax.broadcasted_iota(jnp.int32, (queries.shape[0], key_block.shape[0]), 1)
    return jnp.where(cols_at <= rows_at, scores, NEG_FILL)

def key_blocks_of(keys_all, values_all):
    length = keys_all.shape[0]
    block_rows = min(512, length)
    block_count = length // block_rows
    key_blocks = keys_all.reshape((block_count, block_rows) + keys_all.shape[1:])
    value_blocks = values_all.reshape((block_count, block_rows) + values_all.shape[1:])
    starts = jnp.arange(block_count, dtype=jnp.int32) * block_rows
    return (key_blocks, value_blocks, starts)

def attend(queries, keys_all, values_all, query_start):
    key_blocks, value_blocks, starts = key_blocks_of(keys_all, values_all)
    stat_shape = (queries.shape[1], queries.shape[2], queries.shape[0])

    def gather_stats(carried, pieces):
        running_max, running_sum = carried
        key_block, key_start = pieces
        scores = block_scores(queries, key_block, query_start, key_start)
        new_max = jnp.maximum(running_max, lax.optimization_barrier(jnp.max(scores, axis=-1)))
        new_sum = running_sum * jnp.exp(running_max - new_max) + lax.optimization_barrier(jnp.sum(jnp.exp(scores - new_max[..., None]), axis=-1))
        return ((new_max, new_sum), None)
    initial = (jnp.full(stat_shape, NEG_FILL, jnp.float32), jnp.zeros(stat_shape, jnp.float32))
    row_max, row_sum = lax.scan(gather_stats, initial, (key_blocks, starts))[0]
    log_total = row_max + jnp.log(row_sum)

    def weigh(running, pieces):
        key_block, value_block, key_start = pieces
        scores = block_scores(queries, key_block, query_start, key_start)
        weights = jnp.exp(scores - log_total[..., None]).astype(jnp.bfloat16)
        return (running + jnp.einsum('kgij,jkd->ikgd', weights.astype(jnp.float32), value_block.astype(jnp.float32)), None)
    attended = lax.scan(weigh, jnp.zeros(queries.shape, jnp.float32), (key_blocks, value_blocks, starts))[0]
    return (attended, log_total)

def key_block_grads(queries, key_block, value_block, query_start, key_start, log_total, upstream, centering):
    scores = block_scores(queries, key_block, query_start, key_start)
    probs = jnp.exp(scores - log_total[..., None])
    weights = probs.astype(jnp.bfloat16).astype(jnp.float32)
    upstream_wide = upstream.astype(jnp.float32)
    value_grad = jnp.einsum('kgij,ikgd->jkd', weights, upstream_wide)
    weight_grad = jnp.einsum('ikgd,jkd->kgij', upstream_wide, value_block.astype(jnp.float32))
    score_grad = (probs * (weight_grad - centering[..., None])).astype(jnp.bfloat16).astype(jnp.float32)
    scaling = queries.shape[-1] ** (-0.5)
    query_grad = jnp.einsum('kgij,jkd->ikgd', score_grad, key_block.astype(jnp.float32)) * scaling
    key_grad = jnp.einsum('kgij,ikgd->jkd', score_grad, queries.astype(jnp.float32)) * scaling
    return (query_grad, key_grad, value_grad)

def attention_grads(queries, keys_all, values_all, query_start, log_total, upstream, centering):
    key_blocks, value_blocks, starts = key_blocks_of(keys_all, values_all)

    def step_grads(running, pieces):
        key_block, value_block, key_start = pieces
        query_grad, key_grad, value_grad = key_block_grads(queries, key_block, value_block, query_start, key_start, log_total, upstream, centering)
        return (running + query_grad, (key_grad, value_grad))
    query_total, stacked = lax.scan(step_grads, jnp.zeros(queries.shape, jnp.float32), (key_blocks, value_blocks, starts))
    return (query_total, stacked[0].reshape(keys_all.shape), stacked[1].reshape(values_all.shape))

def attention_sequence(queries_in, keys_in, values_in, gates_in, cotangent_in):
    group_size = AHEADS // KVHEADS
    block_count = LENGTH // TOK_DEV
    shape_five = (block_count, TOK_DEV, KVHEADS, group_size, AD)
    keys_all = keys_in.reshape(LENGTH, KVHEADS, AD)
    values_all = values_in.reshape(LENGTH, KVHEADS, AD)

    def per_block(running, pieces):
        block_queries, block_gates, block_cotangent, block_index = pieces
        query_start = block_index * TOK_DEV
        attended, log_total = attend(block_queries, keys_all, values_all, query_start)
        opening = jax.nn.sigmoid(block_gates.astype(jnp.float32))
        cotangent_wide = block_cotangent.astype(jnp.float32)
        output = (attended * opening).astype(jnp.bfloat16)
        upstream = (cotangent_wide * opening).astype(jnp.bfloat16)
        gate_grad = (cotangent_wide * attended * opening * (1.0 - opening)).astype(jnp.bfloat16)
        centering = jnp.transpose(lax.optimization_barrier(jnp.sum(upstream.astype(jnp.float32) * attended, axis=-1)), (1, 2, 0))
        query_grad, key_grad, value_grad = attention_grads(block_queries, keys_all, values_all, query_start, log_total, upstream, centering)
        return ((running[0] + key_grad, running[1] + value_grad), (output, query_grad.astype(jnp.bfloat16), gate_grad))
    initial = (jnp.zeros((LENGTH, KVHEADS, AD), jnp.float32), jnp.zeros((LENGTH, KVHEADS, AD), jnp.float32))
    pieces = (queries_in.reshape(shape_five), gates_in.reshape(shape_five), cotangent_in.reshape(shape_five), jnp.arange(block_count, dtype=jnp.int32))
    sums, outputs = lax.scan(per_block, initial, pieces)
    flat = (LENGTH, AHEADS * AD)
    return (outputs[0].reshape(flat), outputs[1].reshape(flat), sums[0].reshape(LENGTH, KVHEADS * AD).astype(jnp.bfloat16), sums[1].reshape(LENGTH, KVHEADS * AD).astype(jnp.bfloat16), outputs[2].reshape(flat))

def reference(delta_query, delta_key, delta_value, beta_logit, decay_input, decay_log, norm_gain, output_gate, delta_cotangent, attn_query, attn_key, attn_value, attn_gate, attn_cotangent):
    blank_state = jnp.zeros((DHEADS, DK, DK), jnp.float32)

    def by_heads(array):
        return array.astype(jnp.float32).reshape(LENGTH, DHEADS, DK)

    def layer_only(queries, keys_in, values, beta_in, decay_in, decay_rates, gain_in, gate_values):
        return delta_layer(blank_state, queries, keys_in, values, beta_in, decay_in, decay_rates, gain_in, gate_values, BLOCK_LEN)[0]
    flat = (LENGTH, DHEADS * DK)
    delta_rows, query_rows, key_rows, value_rows, beta_rows, decay_rows, gate_rows = ([], [], [], [], [], [], [])
    log_grad = jnp.zeros((DHEADS,), jnp.float32)
    gain_grad = jnp.zeros((DK,), jnp.float32)
    attn_rows, attn_query_rows, attn_key_rows, attn_value_rows, attn_gate_rows = ([], [], [], [], [])
    for sequence in range(SEQS):
        result, pullback = jax.vjp(layer_only, by_heads(delta_query[sequence]), by_heads(delta_key[sequence]), by_heads(delta_value[sequence]), beta_logit[sequence], decay_input[sequence], decay_log, norm_gain, by_heads(output_gate[sequence]))
        gradients = pullback(by_heads(delta_cotangent[sequence]))
        delta_rows.append(result.reshape(flat).astype(jnp.bfloat16))
        query_rows.append(gradients[0].reshape(flat).astype(jnp.bfloat16))
        key_rows.append(gradients[1].reshape(flat).astype(jnp.bfloat16))
        value_rows.append(gradients[2].reshape(flat).astype(jnp.bfloat16))
        beta_rows.append(gradients[3])
        decay_rows.append(gradients[4])
        log_grad = log_grad + gradients[5]
        gain_grad = gain_grad + gradients[6]
        gate_rows.append(gradients[7].reshape(flat).astype(jnp.bfloat16))
        attn_parts = attention_sequence(attn_query[sequence], attn_key[sequence], attn_value[sequence], attn_gate[sequence], attn_cotangent[sequence])
        attn_rows.append(attn_parts[0])
        attn_query_rows.append(attn_parts[1])
        attn_key_rows.append(attn_parts[2])
        attn_value_rows.append(attn_parts[3])
        attn_gate_rows.append(attn_parts[4])
    return (jnp.stack(delta_rows), jnp.stack(query_rows), jnp.stack(key_rows), jnp.stack(value_rows), jnp.stack(beta_rows), jnp.stack(decay_rows), log_grad, gain_grad, jnp.stack(gate_rows), jnp.stack(attn_rows), jnp.stack(attn_query_rows), jnp.stack(attn_key_rows), jnp.stack(attn_value_rows), jnp.stack(attn_gate_rows))
```

```python
import functools
import jax
import jax.numpy as jnp
from jax import lax
from jax.experimental import pallas as pl
from jax.experimental.pallas import tpu as pltpu
from jax.sharding import PartitionSpec as P

AD = 256
F32 = jnp.float32
BF = jnp.bfloat16
HIGHEST = lax.Precision.HIGHEST
DECAY_FLOOR = -110.0
NEG_FILL = -1e30
KQ = F32
INV = F32
SCO = F32
UPD = F32
KRE = F32
DY = F32
DX = F32
GDX = F32
MK = F32
OUTER = F32
VMEM_LIMIT = 20 << 20


def plain_dot(a, b, ca, cb, precision=None):
    return lax.dot_general(
        a, b, (((ca,), (cb,)), ((), ())), preferred_element_type=F32, precision=precision
    )


def halves(x):
    high = x.astype(BF)
    return high, (x - high.astype(F32)).astype(BF)


def dot(a, b, ca=1, cb=0, precision=None):
    wide_a, wide_b = a.dtype == F32, b.dtype == F32
    if precision is not None or not (wide_a or wide_b):
        return plain_dot(a, b, ca, cb, precision)
    ah, al = halves(a) if wide_a else (a, a)
    bh, bl = halves(b) if wide_b else (b, b)
    if not wide_a:
        return plain_dot(jnp.concatenate([a, a], ca), jnp.concatenate([bh, bl], cb), ca, cb)
    first = plain_dot(jnp.concatenate([ah, al], ca), jnp.concatenate([bh, bh], cb), ca, cb)
    return first + plain_dot(ah, bl, ca, cb) if wide_b else first


def mm3(a, b):
    return dot(a, b)


def interleave(steps):
    steps = list(steps)
    while steps:
        steps = [step for step in steps if next(step, step) is not step]


def ids(rows, cols):
    return (
        lax.broadcasted_iota(jnp.int32, (rows, cols), 0),
        lax.broadcasted_iota(jnp.int32, (rows, cols), 1),
    )


def head_cols(base, slot, width):
    return pl.ds(pl.multiple_of((base ^ slot) * width, width), width)


def unit_of(x):
    inv = lax.rsqrt(jnp.sum(x * x, axis=-1, keepdims=True) + 1e-06)
    return x * inv, inv


def slot_matrix(base, heads, lanes):
    row, col = ids(lanes, lanes)
    return jnp.where((row == (col ^ base)) & (col < heads), 1.0, 0.0).astype(F32)


def softplus(x):
    return jnp.maximum(x, 0.0) + jnp.log(1.0 + jnp.exp(-jnp.abs(x)))


def sigmoid(x):
    return 1.0 / (1.0 + jnp.exp(-x))


def rate_of(log_ref, heads):
    row, col = ids(heads, heads)
    return jnp.sum(jnp.where(row == col, -jnp.exp(log_ref[...]), 0.0), axis=1, keepdims=True)


def fetch(sources, targets, sems):
    copies = [
        pltpu.make_async_copy(source, target, sems.at[i])
        for i, (source, target) in enumerate(zip(sources, targets))
    ]
    for copy in copies:
        copy.start()
    return copies


def fetch_all(sources, targets, sems):
    for copy in fetch(sources, targets, sems):
        copy.wait()


def prepare_kernel(heads, base_ref, *refs):
    sources, refs = refs[:6], refs[6:]
    inputs, sems = refs[15:21], refs[21]
    copies = fetch(sources, inputs, sems)
    q_ref, k_ref, v_ref, beta_ref, decay_ref, log_ref = inputs
    refs = refs[:15]
    half = heads // 2
    base = (base_ref[0] & 1) * (heads // 2)
    g_ref, b_ref, pad = refs[12:]
    perm = slot_matrix(base, heads, pad.shape[0])
    pad[...] = jnp.zeros_like(pad)
    for copy in copies[3:]:
        copy.wait()
    pad[:heads, :] = sigmoid(beta_ref[...])
    b_ref[...] = dot(pad[...], perm, 0, 0, precision=HIGHEST)
    pad[:heads, :] = jnp.maximum(rate_of(log_ref, heads) * softplus(decay_ref[...]), DECAY_FLOOR)
    decays = dot(pad[...], perm, 0, 0, precision=HIGHEST)
    rows = g_ref.shape[0]
    size = refs[1].shape[2]
    row, col = ids(rows, rows)
    within = row >= col
    strict = row > col
    g_all = dot(jnp.where(within, 1.0, 0.0).astype(F32), decays, precision=HIGHEST)
    g_ref[...] = g_all
    betas = b_ref[...]
    g_rows = g_all.T
    identity = jnp.where(row == col, 1.0, 0.0).astype(F32)
    small = 16
    copies[0].wait()
    copies[1].wait()
    units, lowers, inverses = [], [], []

    def begin(s):
        _, kb_ref, qb_ref, _, p_ref, n_ref = refs[6 * (s // half) : 6 * (s // half) + 6]
        i = s % half
        cols = head_cols(base, s, size)
        unit_q = unit_of(q_ref[:, cols].astype(F32))[0] * (size**-0.5)
        unit_k = unit_of(k_ref[:, cols].astype(F32))[0]
        qb = unit_q.astype(KQ)
        kb = unit_k.astype(KQ)
        qb_ref[i] = qb
        kb_ref[i] = kb
        yield
        fade = jnp.exp(jnp.where(within, g_all[:, s : s + 1] - g_rows[s : s + 1, :], 0.0))
        both = dot(jnp.concatenate([kb, qb], 0), kb, 1, 1)
        yield
        plain = jnp.where(strict, fade * both[:rows], 0.0)
        n_ref[i] = plain.astype(n_ref.dtype)
        p_ref[i] = jnp.where(within, fade * both[rows:], 0.0).astype(SCO)
        lower = betas[:, s : s + 1] * plain
        lowers.append(lower)
        diag = jnp.where((row // small) == (col // small), lower, 0.0)
        units.append(diag)
        inverses.append(identity - diag)

    interleave(begin(s) for s in range(heads))
    span = 2
    while span < small:
        units = [mm3(x, x) for x in units]
        inverses = [x + mm3(x, y) for x, y in zip(inverses, units)]
        span *= 2
    span = small
    while span < rows:
        pick = ((row // (2 * span)) == (col // (2 * span))) & ((row // span) != (col // span))
        inner = [mm3(jnp.where(pick, x, 0.0), y) for x, y in zip(lowers, inverses)]
        inverses = [x - mm3(x, y) for x, y in zip(inverses, inner)]
        span *= 2
    row_k, col_k = ids(size, size)
    copies[2].wait()

    def finish(s):
        maps_ref, kb_ref, _, m_ref, _, _ = refs[6 * (s // half) : 6 * (s // half) + 6]
        i = s % half
        cols = head_cols(base, s, size)
        gc = g_all[:, s : s + 1]
        beta = betas[:, s : s + 1]
        end = g_rows[s : s + 1, rows - 1 : rows]
        unit_k = kb_ref[i].astype(F32)
        mb = inverses[s].astype(INV)
        m_ref[i] = mb
        right = jnp.concatenate(
            [(beta * jnp.exp(gc) * unit_k).astype(OUTER), (beta * v_ref[:, cols].astype(F32)).astype(OUTER)], 1
        )
        parts = dot(mb, right)
        yield
        tail = (jnp.exp(end - gc) * unit_k).astype(OUTER)
        both = dot(tail, parts.astype(OUTER), 0, 0)
        yield
        carry = jnp.where(row_k == col_k, jnp.exp(end), 0.0) - both[:, :size]
        maps_ref[i] = jnp.concatenate([carry, both[:, size:]], 1).astype(BF)

    interleave(finish(s) for s in range(heads))


def precise(carry, state, ca=1):
    high, low = halves(state)
    return dot(carry, high, ca, 0) + dot(carry, low, ca, 0)


def bit_of(here_ref, level):
    return (here_ref[0] >> level) & 1


def up_kernel(level, here_ref, own_ref, recv_ref, pair_ref, total_ref):
    bit = bit_of(here_ref, level)
    size = own_ref.shape[1]
    pair_ref[bit] = own_ref[...]
    pair_ref[1 - bit] = recv_ref[...]
    full = total_ref.shape[2] > size
    for i in range(own_ref.shape[0]):
        low, high = pair_ref[0, i], pair_ref[1, i]
        moved = dot(high[:, :size], low if full else low[:, size:])
        if full:
            total_ref[i, :, :size] = moved[:, :size].astype(BF)
            moved = moved[:, size:]
        total_ref[i, :, total_ref.shape[2] - size :] = (
            moved + high[:, size:].astype(F32)
        ).astype(BF)


def down_kernel(levels, here_ref, top_ref, *refs):
    pairs, (own_ref, send_ref) = refs[:-2], refs[-2:]
    size = top_ref.shape[1]

    def one(i):
        state = jnp.where(bit_of(here_ref, levels - 1) == 1, top_ref[i].astype(F32), 0.0)
        for level in range(levels - 2, -1, -1):
            low = pairs[level][0, i]
            later = precise(low[:, :size], state) + low[:, size:].astype(F32)
            yield
            first = bit_of(here_ref, level) == 0
            if level:
                state = jnp.where(first, state, later)
        own_ref[i] = jnp.where(first, state, later).astype(BF)
        send_ref[i] = jnp.where(first, later, state).astype(BF)

    interleave(one(i) for i in range(top_ref.shape[0]))


def up_back_kernel(
    level, count, here_ref, pair_ref, own_ref, recv_ref, mine_ref, locals_ref, total_ref
):
    bit = bit_of(here_ref, level)
    size = pair_ref.shape[2]
    locals_ref[bit] = own_ref[...]
    locals_ref[1 - bit] = recv_ref[...]
    for i in range(count):
        part = pl.ds(i * size, size)
        moved = dot(pair_ref[0, i][:, :size], locals_ref[1, part, :], 0, 0)
        total_ref[part, :] = (moved + locals_ref[0, part, :].astype(F32)).astype(BF)
    add_gain(total_ref, count * size, mine_ref, recv_ref)


def gain_rows(value):
    high, low = halves(value)
    row = lax.broadcasted_iota(jnp.int32, (16, value.shape[1]), 0)
    high, low = high.astype(F32), low.astype(F32)
    return jnp.where(row == 0, high, jnp.where(row == 1, low, 0.0)).astype(BF)


def gain_of(ref, start):
    return jnp.sum(ref[start : start + 16, :].astype(F32), axis=0, keepdims=True)


def add_gain(out_ref, start, own_ref, recv_ref):
    out_ref[start : start + 16, :] = gain_rows(gain_of(own_ref, start) + gain_of(recv_ref, start))


def down_back_kernel(levels, count, here_ref, mine_ref, top_ref, *refs):
    pairs, locals_ = refs[: levels - 1], refs[levels - 1 : 2 * levels - 2]
    own_ref, send_ref, gain_ref = refs[2 * levels - 2 :]
    size = own_ref.shape[1]

    def one(i):
        part = pl.ds(i * size, size)
        state = jnp.where(bit_of(here_ref, levels - 1) == 0, top_ref[part, :].astype(F32), 0.0)
        for level in range(levels - 2, -1, -1):
            earlier = precise(pairs[level][1, i][:, :size], state, 0) + locals_[level][
                1, part, :
            ].astype(F32)
            yield
            first = bit_of(here_ref, level) == 0
            if level:
                state = jnp.where(first, earlier, state)
        own_ref[i] = jnp.where(first, earlier, state).astype(BF)
        send_ref[i] = jnp.where(first, state, earlier).astype(BF)

    interleave(one(i) for i in range(count))
    gain_ref[...] = gain_of(mine_ref, count * size) + gain_of(top_ref, count * size)


def fixed_cols(i, size):
    return slice(i * size, (i + 1) * size)


def output_kernel(
    heads, first, base_ref, state_ref, v_ref, gate_ref, cot_ref, gain_ref, kb_ref, qb_ref, m_ref,
    p_ref, g_ref, b_ref, *refs,
):
    local_ref, u_ref, kre_ref, dy_ref, dx_ref, dg_ref, total_ref, out_ref, dgate_ref = refs[-9:]
    half = heads // 2
    base = (base_ref[0] & 1) * (heads // 2)
    rows = u_ref.shape[1]
    size = kb_ref.shape[2]
    gain = gain_ref[...]
    totals = []
    dg_ref[...] = jnp.zeros_like(dg_ref)

    def one(i):
        s = first + i
        cols, fixed = head_cols(base, s, size), fixed_cols(i, size)
        kb, qb = kb_ref[i], qb_ref[i]
        eg = jnp.exp(g_ref[:, s : s + 1])
        beta = b_ref[:, s : s + 1]
        both = dot(jnp.concatenate([kb, qb], 0), state_ref[i])
        yield
        kre = (eg * both[:rows]).astype(KRE)
        qre = eg * both[rows:]
        kre_ref[i] = kre
        rest = beta * (v_ref[:, cols].astype(F32) - kre.astype(F32))
        mb, pb = m_ref[i], p_ref[i]
        update = dot(mb, rest.astype(UPD)).astype(UPD)
        yield
        u_ref[i] = update
        mix = qre + dot(pb, update)
        yield
        inv = lax.rsqrt(jnp.mean(mix * mix, axis=-1, keepdims=True) + 1e-06)
        norm = mix * inv
        gate = gate_ref[:, cols].astype(F32)
        opening = sigmoid(gate)
        silu = gate * opening
        cot = cot_ref[:, cols].astype(F32)
        normed = norm * gain
        out_ref[:, fixed] = (normed * silu).astype(BF)
        dgate_ref[:, fixed] = (
            cot * normed * (opening * (1.0 + gate * (1.0 - opening)))
        ).astype(BF)
        weighted = cot * silu
        totals.append(jnp.sum(weighted * norm, axis=0, keepdims=True))
        dnorm = weighted * gain
        dmix = inv * (dnorm - norm * jnp.mean(dnorm * norm, axis=-1, keepdims=True))
        dy = dmix.astype(DY)
        dy_ref[i] = dy
        dg_ref[:, s : s + 1] = jnp.sum(qre * dmix, axis=-1, keepdims=True)
        yield
        moved = dot(pb, dy, 0, 0).astype(DX)
        yield
        dx = dot(mb, moved, 0, 0)
        yield
        dx_ref[i] = dx
        left = jnp.concatenate([qb, kb], 0)
        right = jnp.concatenate(
            [(eg * dmix).astype(OUTER), (-(eg * beta) * dx).astype(OUTER)], 0
        )
        local_ref[pl.ds(i * size, size), :] = dot(left, right, 0, 0).astype(BF)

    interleave(one(i) for i in range(half))
    total = sum(totals[1:], totals[0])
    if len(refs) > 9:
        total = total + refs[0][...]
    total_ref[...] = total
    local_ref[half * size : half * size + 16, :] = gain_rows(total)


def query_kernel(heads, base_ref, q_ref, g_ref, *refs):
    half = heads // 2
    dgc_ref, dgr_ref, dq_ref = refs[-3:]
    base = (base_ref[0] & 1) * (heads // 2)
    rows = dq_ref.shape[0]
    size = refs[0].shape[2]
    row, col = ids(rows, rows)
    within = row >= col
    g_all = g_ref[...]
    g_rows = g_all.T
    dgc_ref[...] = refs[7][...] + refs[15][...]
    dgr_ref[...] = jnp.zeros_like(dgr_ref)

    def one(s):
        i, side = s % half, s // half
        state_ref, kb_ref, qb_ref, m_ref, p_ref, u_ref, dy_ref, _ = refs[8 * side : 8 * side + 8]
        dkp_ref, mk_ref = refs[16 + 2 * side : 18 + 2 * side]
        cols = head_cols(base, s, size)
        kb, qb, dy, pb = kb_ref[i], qb_ref[i], dy_ref[i], p_ref[i]
        gc = g_all[:, s : s + 1]
        end = g_rows[s : s + 1, rows - 1 : rows]
        fade = jnp.exp(jnp.where(within, gc - g_rows[s : s + 1, :], 0.0))
        dp = dot(dy, u_ref[i], 1, 1)
        yield
        dpf = jnp.where(within, dp * fade, 0.0).astype(BF)
        moved = dp * pb.astype(F32)
        dgc_ref[:, s : s + 1] += jnp.sum(moved, axis=1, keepdims=True)
        dgr_ref[s : s + 1, :] = -jnp.sum(moved, axis=0, keepdims=True)
        left = jnp.concatenate([(jnp.exp(gc) * dy.astype(F32)).astype(BF), dpf], 1)
        right = jnp.concatenate([state_ref[i].T, kb.astype(BF)], 0)
        dunit = dot(left, right)
        yield
        unit, inv = unit_of(q_ref[:, cols].astype(F32))
        dq_ref[:, cols] = (
            (inv * size**-0.5) * (dunit - unit * jnp.sum(unit * dunit, axis=-1, keepdims=True))
        ).astype(BF)
        dkp_ref[i] = dot(dpf, qb.astype(BF), 0, 0)
        tail = (jnp.exp(end - gc) * kb.astype(F32)).astype(MK)
        mk_ref[i] = dot(m_ref[i], tail, 0, 0).astype(MK)
        yield

    interleave(one(s) for s in range(heads))


def decay_kernel(
    heads, first, final, base_ref, state_ref, grad_ref, k_ref, v_ref, n_ref, g_ref, b_ref, u_ref, kre_ref,
    dx_ref, mk_ref, dgc_in, dgr_in, *refs,
):
    if not final:
        dmat_ref, dtail_ref, gdv_ref, dgc, dgr, dbc, dv_ref = refs
        dgc[...] = dgc_in[...]
        dgr[...] = dgr_in[...]
        dbc[...] = jnp.zeros_like(dbc)
    else:
        (
            decay_ref, log_ref, dbc_far, gain_ref, _, dmat_ref, dtail_ref, gdv_ref, dbeta_ref,
            ddecay_ref, small_ref, dv_ref, dgc, dgr, dbc, pad,
        ) = refs
        dgc[...] = dgc_in[...]
        dgr[...] = dgr_in[...]
        dbc[...] = dbc_far[...]
    base = (base_ref[0] & 1) * (heads // 2)
    rows = dv_ref.shape[0]
    size = mk_ref.shape[2]
    lanes = g_ref.shape[1]
    row, col = ids(rows, rows)
    within = row >= col
    strict = row > col
    last = lax.broadcasted_iota(jnp.int32, (rows, 1), 0) == rows - 1
    g_all = g_ref[...]
    g_rows = g_all.T

    def one(i):
        s = first + i
        cols = head_cols(base, s, size)
        update = u_ref[i]
        gc = g_all[:, s : s + 1]
        beta = b_ref[:, s : s + 1]
        end = g_rows[s : s + 1, rows - 1 : rows]
        state, grad = state_ref[i], grad_ref[i]
        fade = jnp.exp(jnp.where(within, gc - g_rows[s : s + 1, :], 0.0))
        dx = dx_ref[i] + dot(mk_ref[i], grad)
        yield
        kre = kre_ref[i].astype(F32)
        dv = beta * dx
        dv_ref[:, fixed_cols(i, size)] = dv.astype(BF)
        gdv_ref[i] = (-jnp.exp(gc) * dv).astype(BF)
        da = jnp.where(strict, -dot(dx.astype(GDX), update, 1, 1), 0.0)
        yield
        by_beta = da * n_ref[i].astype(F32)
        moved = beta * by_beta
        dbc[:, s : s + 1] = jnp.sum(
            by_beta + dx * (v_ref[:, cols].astype(F32) - kre), axis=1, keepdims=True
        )
        dmat_ref[i] = (da * (beta * fade)).astype(BF)
        dtail = jnp.exp(end - gc) * dot(update, grad, 1, 1)
        yield
        dtail_ref[i] = dtail
        unit = unit_of(k_ref[:, cols].astype(F32))[0]
        ends = dtail * unit
        dend = jnp.sum(
            jnp.sum(ends, axis=0, keepdims=True)
            + jnp.exp(end)
            * jnp.sum(state.astype(F32) * grad.astype(F32), axis=0, keepdims=True),
            axis=1,
            keepdims=True,
        )
        dgc[:, s : s + 1] = (
            dgc[:, s : s + 1]
            + jnp.sum(moved - ends - kre * dv, axis=1, keepdims=True)
            + jnp.where(last, dend, 0.0)
        )
        dgr[s : s + 1, :] = dgr[s : s + 1, :] - jnp.sum(moved, axis=0, keepdims=True)

    interleave(one(i) for i in range(heads // 2))
    if not final:
        return
    perm = slot_matrix(base, heads, lanes)
    ahead = jnp.where(row <= col, 1.0, 0.0).astype(F32)
    ddecay = dot(
        perm, dot(ahead, dgc[...] + dgr[...].T, precision=HIGHEST), 1, 1, precision=HIGHEST
    )[:heads]
    betas = b_ref[...]
    dbeta = dot(perm, dbc[...] * betas * (1.0 - betas), 1, 1, precision=HIGHEST)
    dbeta_ref[...] = dbeta[:heads]
    rate = rate_of(log_ref, heads)
    inputs = decay_ref[...]
    ddecay_ref[...] = ddecay * rate * sigmoid(inputs)
    pad[...] = jnp.zeros_like(pad)
    pad[:heads, :] = ddecay * rate * softplus(inputs)
    small_ref[0:1, :] = jnp.sum(pad[...].T, axis=0, keepdims=True)
    small_ref[1:2, :] = gain_ref[...]


def key_kernel(heads, base_ref, k_ref, *refs):
    half = heads // 2
    dk_ref = refs[-1]
    base = (base_ref[0] & 1) * (heads // 2)
    size = refs[0].shape[2]

    def one(s):
        i, side = s % half, s // half
        state_ref, kb_ref, dkp_ref, gdv_ref, dmat_ref, dtail_ref = refs[6 * side : 6 * side + 6]
        cols = head_cols(base, s, size)
        dmat = dmat_ref[i].astype(F32)
        left = jnp.concatenate([(dmat + dmat.T).astype(BF), gdv_ref[i]], 1)
        right = jnp.concatenate([kb_ref[i].astype(BF), state_ref[i].T], 0)
        yield
        dunit = dkp_ref[i] + dot(left, right) + dtail_ref[i]
        yield
        unit, inv = unit_of(k_ref[:, cols].astype(F32))
        dk_ref[:, cols] = (
            inv * (dunit - unit * jnp.sum(unit * dunit, axis=-1, keepdims=True))
        ).astype(BF)

    interleave(one(s) for s in range(heads))


def pair_kernel(_, first_ref, second_ref, out_ref, sems):
    cut = first_ref.shape[1]
    fetch_all((first_ref, second_ref), (out_ref.at[0, :, :cut], out_ref.at[0, :, cut:]), sems)


def join_kernel(_, first_ref, second_ref, out_ref):
    cut = first_ref.shape[0]
    out_ref[:cut] = first_ref[...]
    out_ref[cut:] = second_ref[...]


def attention_kernel(offsets, start, end, here_ref, q_ref, gate_ref, cot_ref, near_ref, far_ref, *refs):
    raised_ref, weights_ref, score_ref = refs[-3:]
    if start:
        ins, outs = (), refs[:-3]
    else:
        ins, outs = refs[:3], refs[6:-3]
    out_ref, dq_ref, dgate_ref = outs[:3]
    count = len(offsets)
    half = count // 2
    here = here_ref[0]
    rows = q_ref.shape[0]
    size = near_ref.shape[2] // 2
    group = q_ref.shape[1] // size
    wide = group * rows
    scaling = size**-0.5

    def keys_of(k):
        return (near_ref if k < half else far_ref)[k % half][:, :size]

    def values_of(k):
        return (near_ref if k < half else far_ref)[k % half][:, size:]

    if start:
        keys_t, values_t = outs[3:5]
        for k in range(count):
            part = pl.ds(k * rows, rows)
            keys_t[:, part] = keys_of(k).T
            values_t[:, part] = values_of(k).T
    else:
        keys_t, values_t, total_in = ins

    def stack(ref):
        return jnp.concatenate([ref[:, i * size : (i + 1) * size] for i in range(group)], 0)

    def spread(ref, value):
        for i in range(group):
            ref[:, i * size : (i + 1) * size] = value[i * rows : (i + 1) * rows].astype(ref.dtype)

    queries = (stack(q_ref).astype(F32) * scaling).astype(BF)
    key_at, query_at = ids(rows, wide)
    own = key_at <= (query_at % rows)
    top = jnp.full((1, wide), NEG_FILL, F32)
    biases = [jnp.where((here ^ x) < here, 0.0, NEG_FILL) if x else 0.0 for x in offsets]
    for k in range(count):
        scores = dot(keys_of(k), queries, 1, 1)
        if offsets[k] == 0:
            scores = jnp.where(own, scores, NEG_FILL)
        raised_ref[pl.ds(k * rows, rows), :] = scores
        top = jnp.maximum(top, jnp.max(scores, axis=0, keepdims=True) + biases[k])
    total = jnp.zeros((1, wide), F32)
    for k in range(count):
        part = pl.ds(k * rows, rows)
        raised = jnp.exp(raised_ref[part, :] - (top - biases[k]))
        raised_ref[part, :] = raised
        total = total + jnp.sum(raised, axis=0, keepdims=True)
    scale = 1.0 / total
    for k in range(count):
        part = pl.ds(k * rows, rows)
        weights_ref[part, :] = (raised_ref[part, :] * scale).astype(BF)
    attended_t = dot(values_t[...], weights_ref[...])
    attended = attended_t.T
    gate = stack(gate_ref).astype(F32)
    cot = stack(cot_ref).astype(F32)
    opening = sigmoid(gate)
    spread(out_ref, attended * opening)
    up = (cot * opening).astype(BF)
    spread(dgate_ref, cot * attended * opening * (1.0 - opening))
    up_t = up.T
    centering = jnp.sum(up_t.astype(F32) * attended_t, axis=0, keepdims=True) * scale
    for k in range(count):
        part = pl.ds(k * rows, rows)
        weight_grad = dot(values_of(k), up_t)
        score_ref[part, :] = (raised_ref[part, :] * (weight_grad * scale - centering)).astype(BF)
    dq_t = dot(keys_t[...], score_ref[...]) * scaling
    spread(dq_ref, dq_t.T)
    dk = dot(score_ref[...], queries)
    dv = dot(weights_ref[...], up)
    for k in range(count):
        part = slice(k * rows, (k + 1) * rows)
        if end:
            target, at = (outs[3] if k < half else outs[4]), k % half
        else:
            target, at = outs[-1], k
        dk_part, dv_part = dk[part], dv[part]
        if not start:
            dk_part = dk_part + total_in[k, :, :size]
            dv_part = dv_part + total_in[k, :, size:]
        target[at, :, :size] = dk_part.astype(target.dtype)
        target[at, :, size:] = dv_part.astype(target.dtype)


def call(kernel, outs, scratch, base, *args, blocked=(), prior=None, side=0, far=False):
    vmem = pl.BlockSpec(memory_space=pltpu.VMEM)
    hbm = pl.BlockSpec(memory_space=pl.ANY)
    if far:
        args = tuple(pltpu.with_memory_space_constraint(x, pltpu.HBM) for x in args)
    args = tuple(args) + tuple(prior or ())
    count = len(args) + 1 - len(prior or ())
    return pl.pallas_call(
        kernel,
        out_shape=tuple(jax.ShapeDtypeStruct(shape, dtype) for shape, dtype in tuple(outs) + tuple(blocked)),
        grid_spec=pltpu.PrefetchScalarGridSpec(
            num_scalar_prefetch=1,
            grid=(1,),
            in_specs=[pl.BlockSpec(memory_space=pltpu.HBM) if far else vmem] * (count - 1) + [hbm] * len(prior or ()),
            out_specs=tuple(vmem for _ in outs)
            + tuple(
                pl.BlockSpec((shape[0], shape[1] // 2), lambda i, where: (0, (where[0] & 1) ^ side))
                for shape, _ in blocked
            ),
            scratch_shapes=scratch,
        ),
        input_output_aliases={count + i: len(outs) + i for i in range(len(prior or ()))},
        compiler_params=pltpu.CompilerParams(vmem_limit_bytes=VMEM_LIMIT),
    )(base, *args)


def swap(value, axis, offset):
    count = lax.axis_size(axis)
    return lax.ppermute(value, axis, [(i, i ^ offset) for i in range(count)])


def axis_sum(value, axis):
    offset = 1
    while offset < lax.axis_size(axis):
        value = value + swap(value, axis, offset)
        offset *= 2
    return value


def per_device(
    delta_query,
    delta_key,
    delta_value,
    beta_logit,
    decay_input,
    decay_log,
    norm_gain,
    output_gate,
    delta_cotangent,
    attn_query,
    attn_key,
    attn_value,
    attn_gate,
    attn_cotangent,
):
    tokens = delta_query.shape[1]
    heads = decay_log.shape[0]
    size = norm_gain.shape[0]
    lanes = 128
    count = lax.axis_size("ctx")
    levels = count.bit_length() - 1
    here = lax.axis_index("ctx").astype(jnp.int32)
    half = heads // 2
    spot = here.reshape(1)

    rows_att, key_width = attn_key.shape[1], attn_key.shape[2]
    (near_kv,) = call(
        pair_kernel, [((1, rows_att, 2 * key_width), BF)], [pltpu.SemaphoreType.DMA((2,))],
        spot, attn_key[0], attn_value[0], far=True,
    )
    offsets = [0]
    jump = count // 2
    while jump > 1:
        moved = swap(near_kv, "ctx", jump)
        (near_kv,) = call(
            join_kernel,
            [((2 * near_kv.shape[0],) + near_kv.shape[1:], BF)], [], spot, near_kv, moved,
        )
        offsets += [x ^ jump for x in offsets]
        jump //= 2
    far_kv = swap(near_kv, "ctx", 1)
    offsets += [x ^ 1 for x in offsets]

    q, k, v = delta_query[0], delta_key[0], delta_value[0]
    beta, decay, logs = beta_logit[0].T, decay_input[0].T, decay_log[None]
    column = ((tokens, lanes), F32)
    turned = ((lanes, tokens), F32)
    flat = ((tokens, heads * size), BF)
    small = ((heads, tokens), F32)
    maps = ((half, size, 2 * size), BF)
    states = ((half, size, size), BF)
    cube = ((half, tokens, size), BF)
    cube_wide = ((half, tokens, size), F32)
    square = ((half, tokens, tokens), BF)
    packed = ((half * size + 16, size), BF)
    column_scratch = pltpu.VMEM(*column)

    kept = [maps, (cube[0], KQ), (cube[0], KQ), (square[0], INV), (square[0], SCO), (square[0], SCO)]
    results = call(
        functools.partial(prepare_kernel, heads), kept + kept + [column, column],
        [pltpu.VMEM(*turned)]
        + [pltpu.VMEM(x.shape, x.dtype) for x in (q, k, v, beta, decay, logs)]
        + [pltpu.SemaphoreType.DMA((6,))],
        spot, q, k, v, beta, decay, logs, far=True,
    )
    keep, *near = results[:6]
    send, *far = results[6:12]
    g, b = results[12:]
    pairs = []
    for level in range(levels - 1):
        moved = swap(send, "ctx", 1 << level)
        pair, total = call(
            functools.partial(up_kernel, level),
            [((2,) + maps[0], BF), maps if level < levels - 2 else states],
            [], spot, keep, moved,
        )
        pairs.append(pair)
        keep = send = total
    moved = swap(send, "ctx", 1 << (levels - 1))
    near_state, send = call(
        functools.partial(down_kernel, levels), [states, states], [], spot, moved, *pairs
    )
    far_state = swap(send, "ctx", 1)
    gain = norm_gain[None]
    gates = output_gate[0], delta_cotangent[0], gain
    kept = [packed, (cube[0], UPD), (cube[0], KRE), (cube[0], DY), cube_wide, column, ((1, size), F32)]
    keep, *near_out, dg_near, gain_near, out, dgate = call(
        functools.partial(output_kernel, heads, 0), kept, [],
        spot, near_state, v, *gates, near[0], near[1], near[2], near[3], g, b,
        blocked=[flat, flat],
    )
    send, *far_out, dg_far, _, out, dgate = call(
        functools.partial(output_kernel, heads, half), kept, [],
        spot, far_state, v, *gates, far[0], far[1], far[2], far[3], g, b, gain_near,
        blocked=[flat, flat], prior=[out, dgate], side=1,
    )
    locals_ = []
    for level in range(levels - 1):
        moved = swap(send, "ctx", 1 << level)
        both, total = call(
            functools.partial(up_back_kernel, level, half),
            [((2,) + packed[0], BF), packed],
            [], spot, pairs[level], keep, moved, send,
        )
        locals_.append(both)
        keep = send = total
    moved = swap(send, "ctx", 1 << (levels - 1))
    near_grad, send, gain_part = call(
        functools.partial(down_back_kernel, levels, half), [states, states, ((1, size), F32)], [],
        spot, keep, moved, *pairs, *locals_,
    )
    far_grad = swap(send, "ctx", 1)
    gain_part = axis_sum(gain_part, "head")
    dkp_near, mk_near, dkp_far, mk_far, dgc, dgr, dq = call(
        functools.partial(query_kernel, heads),
        [cube_wide, (cube[0], MK), cube_wide, (cube[0], MK), column, turned, flat], [], spot, q, g,
        near_state, near[0], near[1], near[2], near[3], near_out[0], near_out[2], dg_near,
        far_state, far[0], far[1], far[2], far[3], far_out[0], far_out[2], dg_far,
    )
    dmat_near, dtail_near, gdv_near, dgc, dgr, dbc, dv = call(
        functools.partial(decay_kernel, heads, 0, False),
        [square, cube_wide, cube, column, turned, column], [],
        spot, near_state, near_grad, k, v, near[4], g, b, near_out[0], near_out[1], near_out[3],
        mk_near, dgc, dgr,
        blocked=[flat],
    )
    dmat_far, dtail_far, gdv_far, dbeta, ddecay, sums, dv = call(
        functools.partial(decay_kernel, heads, half, True),
        [square, cube_wide, cube, small, small, ((2, lanes), F32)],
        [column_scratch, pltpu.VMEM(*turned), column_scratch, column_scratch],
        spot, far_state, far_grad, k, v, far[4], g, b, far_out[0], far_out[1], far_out[3],
        mk_far, dgc, dgr, decay, logs, dbc, gain_part,
        blocked=[flat], prior=[dv], side=1,
    )
    (dk,) = call(
        functools.partial(key_kernel, heads), [flat], [], spot, k,
        near_state, near[0], dkp_near, gdv_near, dmat_near, dtail_near,
        far_state, far[0], dkp_far, gdv_far, dmat_far, dtail_far,
    )
    sums = axis_sum(sums, "section")
    gain_grad = sums[1]
    log_grad = sums[:1]
    for level in range(levels):
        log_grad = log_grad + swap(log_grad, "ctx", 1 << level)

    groups = attn_query.shape[2] // AD
    group = 2 if groups % 2 == 0 else 1
    calls = groups // group
    length = count * rows_att
    vmem = pl.BlockSpec(memory_space=pltpu.VMEM)
    wide = jax.ShapeDtypeStruct((rows_att, groups * AD), BF)
    turned_kv = jax.ShapeDtypeStruct((AD, length), BF)
    terms = jax.ShapeDtypeStruct((count, rows_att, 2 * key_width), F32)
    extra, outs = [], []
    for j in range(calls):
        start, end = j == 0, j == calls - 1
        block = pl.BlockSpec((rows_att, group * AD), lambda i, where, j=j: (0, j))
        tail = [turned_kv, turned_kv] if start else []
        if end:
            tail = tail + [
                jax.ShapeDtypeStruct(near_kv.shape, F32), jax.ShapeDtypeStruct(near_kv.shape, BF)
            ]
        else:
            tail = tail + [terms]
        results = pl.pallas_call(
            functools.partial(attention_kernel, offsets, start, end),
            grid_spec=pltpu.PrefetchScalarGridSpec(
                num_scalar_prefetch=1,
                grid=(1,),
                in_specs=[block, block, block] + [vmem] * (2 + len(extra))
                + [pl.BlockSpec(memory_space=pl.ANY)] * len(outs),
                out_specs=[block, block, block] + [vmem] * len(tail),
                scratch_shapes=[
                    pltpu.VMEM((length, group * rows_att), dtype) for dtype in (F32, BF, BF)
                ],
            ),
            out_shape=[wide, wide, wide] + tail,
            input_output_aliases={6 + len(extra) + i: i for i in range(len(outs))},
            compiler_params=pltpu.CompilerParams(vmem_limit_bytes=VMEM_LIMIT),
        )(spot, attn_query[0], attn_gate[0], attn_cotangent[0], near_kv, far_kv, *extra, *outs)
        outs = results[:3]
        if start:
            keys_t, values_t = results[3:5]
        extra = [keys_t, values_t, results[-1]]
    attn_out, dquery, dgate_att = outs
    own, send = results[-2:]
    moved = swap(send, "ctx", 1)
    own = own + moved.astype(F32)
    jump = 2
    while jump < count:
        own, send = jnp.split(own, 2)
        send = send.astype(BF)
        moved = swap(send, "ctx", jump)
        own = own + moved.astype(F32)
        jump *= 2
    own = own[0].astype(BF)
    return (
        out[None],
        dq[None],
        dk[None],
        dv[None],
        dbeta.T[None],
        ddecay.T[None],
        log_grad[0, :heads],
        gain_grad,
        dgate[None],
        attn_out[None],
        dquery[None],
        own[:, :key_width][None],
        own[:, key_width:][None],
        dgate_att[None],
    )


def solution(mesh):
    split = P("section", "ctx", "head")
    in_specs = (split,) * 5 + (P("head"), P()) + (split,) * 7
    out_specs = (split,) * 6 + (P("head"), P()) + (split,) * 6

    return jax.shard_map(
        per_device, mesh=mesh, in_specs=in_specs, out_specs=out_specs, check_vma=False
    )
```

```python
import functools
import jax
import jax.numpy as jnp
from jax import lax
from jax.experimental import pallas as pl
from jax.experimental.pallas import tpu as pltpu
from jax.sharding import PartitionSpec as P

AD = 256
F32 = jnp.float32
BF = jnp.bfloat16
HIGHEST = lax.Precision.HIGHEST
DECAY_FLOOR = -110.0
NEG_FILL = -1e30
KQ = F32
INV = F32
SCO = F32
UPD = F32
KRE = F32
DY = F32
DX = F32
GDX = F32
MK = F32
OUTER = BF
VMEM_LIMIT = 20 << 20


def plain_dot(a, b, ca, cb, precision=None):
    return lax.dot_general(
        a, b, (((ca,), (cb,)), ((), ())), preferred_element_type=F32, precision=precision
    )


def halves(x):
    high = x.astype(BF)
    return high, (x - high.astype(F32)).astype(BF)


def dot(a, b, ca=1, cb=0, precision=None):
    wide_a, wide_b = a.dtype == F32, b.dtype == F32
    if precision is not None or not (wide_a or wide_b):
        return plain_dot(a, b, ca, cb, precision)
    ah, al = halves(a) if wide_a else (a, a)
    bh, bl = halves(b) if wide_b else (b, b)
    if not wide_a:
        return plain_dot(jnp.concatenate([a, a], ca), jnp.concatenate([bh, bl], cb), ca, cb)
    first = plain_dot(jnp.concatenate([ah, al], ca), jnp.concatenate([bh, bh], cb), ca, cb)
    return first + plain_dot(ah, bl, ca, cb) if wide_b else first


def mm3(a, b):
    return dot(a, b)


def interleave(steps):
    steps = list(steps)
    while steps:
        steps = [step for step in steps if next(step, step) is not step]


def ids(rows, cols):
    return (
        lax.broadcasted_iota(jnp.int32, (rows, cols), 0),
        lax.broadcasted_iota(jnp.int32, (rows, cols), 1),
    )


def head_cols(base, slot, width):
    return pl.ds(pl.multiple_of((base ^ slot) * width, width), width)


def unit_of(x):
    inv = lax.rsqrt(jnp.sum(x * x, axis=-1, keepdims=True) + 1e-06)
    return x * inv, inv


def slot_matrix(base, heads, lanes):
    row, col = ids(lanes, lanes)
    return jnp.where((row == (col ^ base)) & (col < heads), 1.0, 0.0).astype(F32)


def softplus(x):
    return jnp.maximum(x, 0.0) + jnp.log(1.0 + jnp.exp(-jnp.abs(x)))


def sigmoid(x):
    return 1.0 / (1.0 + jnp.exp(-x))


def rate_of(log_ref, heads):
    row, col = ids(heads, heads)
    return jnp.sum(jnp.where(row == col, -jnp.exp(log_ref[...]), 0.0), axis=1, keepdims=True)


def fetch(sources, targets, sems):
    copies = [
        pltpu.make_async_copy(source, target, sems.at[i])
        for i, (source, target) in enumerate(zip(sources, targets))
    ]
    for copy in copies:
        copy.start()
    return copies


def fetch_all(sources, targets, sems):
    for copy in fetch(sources, targets, sems):
        copy.wait()


def prepare_kernel(heads, base_ref, *refs):
    sources, refs = refs[:5], refs[5:]
    inputs, sems = refs[11:16], refs[16]
    copies = fetch(sources, inputs, sems)
    k_ref, v_ref, beta_ref, decay_ref, log_ref = inputs
    refs = refs[:11]
    half = heads // 2
    base = (base_ref[0] & 1) * (heads // 2)
    g_ref, b_ref, pad = refs[8:]
    perm = slot_matrix(base, heads, pad.shape[0])
    pad[...] = jnp.zeros_like(pad)
    for copy in copies[2:]:
        copy.wait()
    pad[:heads, :] = sigmoid(beta_ref[...])
    b_ref[...] = dot(pad[...], perm, 0, 0, precision=HIGHEST)
    pad[:heads, :] = jnp.maximum(rate_of(log_ref, heads) * softplus(decay_ref[...]), DECAY_FLOOR)
    decays = dot(pad[...], perm, 0, 0, precision=HIGHEST)
    rows = g_ref.shape[0]
    size = refs[1].shape[2]
    row, col = ids(rows, rows)
    within = row >= col
    strict = row > col
    g_all = dot(jnp.where(within, 1.0, 0.0).astype(F32), decays, precision=HIGHEST)
    g_ref[...] = g_all
    betas = b_ref[...]
    g_rows = g_all.T
    identity = jnp.where(row == col, 1.0, 0.0).astype(F32)
    small = 16
    copies[0].wait()
    units, lowers, inverses = [], [], []

    def begin(s):
        _, kb_ref, _, n_ref = refs[4 * (s // half) : 4 * (s // half) + 4]
        i = s % half
        cols = head_cols(base, s, size)
        unit_k = unit_of(k_ref[:, cols].astype(F32))[0]
        kb = unit_k.astype(KQ)
        kb_ref[i] = kb
        yield
        fade = jnp.exp(jnp.where(within, g_all[:, s : s + 1] - g_rows[s : s + 1, :], 0.0))
        both = dot(kb, kb, 1, 1)
        yield
        plain = jnp.where(strict, fade * both, 0.0)
        n_ref[i] = plain.astype(n_ref.dtype)
        lower = betas[:, s : s + 1] * plain
        lowers.append(lower)
        diag = jnp.where((row // small) == (col // small), lower, 0.0)
        units.append(diag)
        inverses.append(identity - diag)

    interleave(begin(s) for s in range(heads))
    span = 2
    while span < small:
        units = [mm3(x, x) for x in units]
        inverses = [x + mm3(x, y) for x, y in zip(inverses, units)]
        span *= 2
    span = small
    while span < rows:
        pick = ((row // (2 * span)) == (col // (2 * span))) & ((row // span) != (col // span))
        inner = [mm3(jnp.where(pick, x, 0.0), y) for x, y in zip(lowers, inverses)]
        inverses = [x - mm3(x, y) for x, y in zip(inverses, inner)]
        span *= 2
    row_k, col_k = ids(size, size)
    copies[1].wait()

    def finish(s):
        maps_ref, kb_ref, m_ref, _ = refs[4 * (s // half) : 4 * (s // half) + 4]
        i = s % half
        cols = head_cols(base, s, size)
        gc = g_all[:, s : s + 1]
        beta = betas[:, s : s + 1]
        end = g_rows[s : s + 1, rows - 1 : rows]
        unit_k = kb_ref[i].astype(F32)
        mb = inverses[s].astype(INV)
        m_ref[i] = mb
        right = jnp.concatenate(
            [(beta * jnp.exp(gc) * unit_k).astype(OUTER), (beta * v_ref[:, cols].astype(F32)).astype(OUTER)], 1
        )
        parts = dot(mb, right)
        yield
        tail = (jnp.exp(end - gc) * unit_k).astype(OUTER)
        both = dot(tail, parts.astype(OUTER), 0, 0)
        yield
        carry = jnp.where(row_k == col_k, jnp.exp(end), 0.0) - both[:, :size]
        maps_ref[i] = jnp.concatenate([carry, both[:, size:]], 1).astype(BF)

    interleave(finish(s) for s in range(heads))


def score_kernel(heads, base_ref, q_ref, g_ref, *refs):
    half = heads // 2
    base = (base_ref[0] & 1) * half
    rows = g_ref.shape[0]
    size = refs[0].shape[2]
    row, col = ids(rows, rows)
    within = row >= col
    g_all = g_ref[...]
    g_rows = g_all.T

    def one(s):
        i, side = s % half, s // half
        kb = refs[side][i]
        qb_ref, p_ref = refs[2 + 2 * side : 4 + 2 * side]
        cols = head_cols(base, s, size)
        qb = (unit_of(q_ref[:, cols].astype(F32))[0] * (size**-0.5)).astype(KQ)
        qb_ref[i] = qb
        yield
        fade = jnp.exp(jnp.where(within, g_all[:, s : s + 1] - g_rows[s : s + 1, :], 0.0))
        products = dot(qb, kb, 1, 1)
        yield
        p_ref[i] = jnp.where(within, fade * products, 0.0).astype(SCO)

    interleave(one(s) for s in range(heads))


def precise(carry, state, ca=1):
    high, low = halves(state)
    return dot(carry, high, ca, 0) + dot(carry, low, ca, 0)


def bit_of(here_ref, level):
    return (here_ref[0] >> level) & 1


def up_kernel(level, here_ref, own_ref, recv_ref, pair_ref, total_ref):
    bit = bit_of(here_ref, level)
    size = own_ref.shape[1]
    pair_ref[bit] = own_ref[...]
    pair_ref[1 - bit] = recv_ref[...]
    full = total_ref.shape[2] > size
    for i in range(own_ref.shape[0]):
        low, high = pair_ref[0, i], pair_ref[1, i]
        moved = dot(high[:, :size], low if full else low[:, size:])
        if full:
            total_ref[i, :, :size] = moved[:, :size].astype(BF)
            moved = moved[:, size:]
        total_ref[i, :, total_ref.shape[2] - size :] = (
            moved + high[:, size:].astype(F32)
        ).astype(BF)


def down_kernel(levels, here_ref, top_ref, *refs):
    pairs, (own_ref, send_ref) = refs[:-2], refs[-2:]
    size = top_ref.shape[1]

    def one(i):
        state = jnp.where(bit_of(here_ref, levels - 1) == 1, top_ref[i].astype(F32), 0.0)
        for level in range(levels - 2, -1, -1):
            low = pairs[level][0, i]
            later = precise(low[:, :size], state) + low[:, size:].astype(F32)
            yield
            first = bit_of(here_ref, level) == 0
            if level:
                state = jnp.where(first, state, later)
        own_ref[i] = jnp.where(first, state, later).astype(BF)
        send_ref[i] = jnp.where(first, later, state).astype(BF)

    interleave(one(i) for i in range(top_ref.shape[0]))


def up_back_kernel(
    level, count, here_ref, pair_ref, own_ref, recv_ref, mine_ref, locals_ref, total_ref
):
    bit = bit_of(here_ref, level)
    size = pair_ref.shape[2]
    locals_ref[bit] = own_ref[...]
    locals_ref[1 - bit] = recv_ref[...]
    for i in range(count):
        part = pl.ds(i * size, size)
        moved = dot(pair_ref[0, i][:, :size], locals_ref[1, part, :], 0, 0)
        total_ref[part, :] = (moved + locals_ref[0, part, :].astype(F32)).astype(BF)
    add_gain(total_ref, count * size, mine_ref, recv_ref)


def gain_rows(value):
    high, low = halves(value)
    row = lax.broadcasted_iota(jnp.int32, (16, value.shape[1]), 0)
    high, low = high.astype(F32), low.astype(F32)
    return jnp.where(row == 0, high, jnp.where(row == 1, low, 0.0)).astype(BF)


def gain_of(ref, start):
    return jnp.sum(ref[start : start + 16, :].astype(F32), axis=0, keepdims=True)


def add_gain(out_ref, start, own_ref, recv_ref):
    out_ref[start : start + 16, :] = gain_rows(gain_of(own_ref, start) + gain_of(recv_ref, start))


def down_back_kernel(levels, count, here_ref, mine_ref, top_ref, *refs):
    pairs, locals_ = refs[: levels - 1], refs[levels - 1 : 2 * levels - 2]
    own_ref, send_ref, gain_ref = refs[2 * levels - 2 :]
    size = own_ref.shape[1]

    def one(i):
        part = pl.ds(i * size, size)
        state = jnp.where(bit_of(here_ref, levels - 1) == 0, top_ref[part, :].astype(F32), 0.0)
        for level in range(levels - 2, -1, -1):
            earlier = precise(pairs[level][1, i][:, :size], state, 0) + locals_[level][
                1, part, :
            ].astype(F32)
            yield
            first = bit_of(here_ref, level) == 0
            if level:
                state = jnp.where(first, earlier, state)
        own_ref[i] = jnp.where(first, earlier, state).astype(BF)
        send_ref[i] = jnp.where(first, state, earlier).astype(BF)

    interleave(one(i) for i in range(count))
    gain_ref[...] = gain_of(mine_ref, count * size) + gain_of(top_ref, count * size)


def fixed_cols(i, size):
    return slice(i * size, (i + 1) * size)


def output_kernel(
    heads, first, base_ref, state_ref, v_ref, gate_ref, cot_ref, gain_ref, kb_ref, qb_ref, m_ref,
    p_ref, g_ref, b_ref, *refs,
):
    local_ref, u_ref, kre_ref, dy_ref, dx_ref, dg_ref, total_ref, out_ref, dgate_ref = refs[-9:]
    half = heads // 2
    base = (base_ref[0] & 1) * (heads // 2)
    rows = u_ref.shape[1]
    size = kb_ref.shape[2]
    gain = gain_ref[...]
    totals = []
    dg_ref[...] = jnp.zeros_like(dg_ref)

    def one(i):
        s = first + i
        cols, fixed = head_cols(base, s, size), fixed_cols(i, size)
        kb, qb = kb_ref[i], qb_ref[i]
        eg = jnp.exp(g_ref[:, s : s + 1])
        beta = b_ref[:, s : s + 1]
        both = dot(jnp.concatenate([kb, qb], 0), state_ref[i])
        yield
        kre = (eg * both[:rows]).astype(KRE)
        qre = eg * both[rows:]
        kre_ref[i] = kre
        rest = beta * (v_ref[:, cols].astype(F32) - kre.astype(F32))
        mb, pb = m_ref[i], p_ref[i]
        update = dot(mb, rest.astype(UPD)).astype(UPD)
        yield
        u_ref[i] = update
        mix = qre + dot(pb, update)
        yield
        inv = lax.rsqrt(jnp.mean(mix * mix, axis=-1, keepdims=True) + 1e-06)
        norm = mix * inv
        gate = gate_ref[:, cols].astype(F32)
        opening = sigmoid(gate)
        silu = gate * opening
        cot = cot_ref[:, cols].astype(F32)
        normed = norm * gain
        out_ref[:, fixed] = (normed * silu).astype(BF)
        dgate_ref[:, fixed] = (
            cot * normed * (opening * (1.0 + gate * (1.0 - opening)))
        ).astype(BF)
        weighted = cot * silu
        totals.append(jnp.sum(weighted * norm, axis=0, keepdims=True))
        dnorm = weighted * gain
        dmix = inv * (dnorm - norm * jnp.mean(dnorm * norm, axis=-1, keepdims=True))
        dy = dmix.astype(DY)
        dy_ref[i] = dy
        dg_ref[:, s : s + 1] = jnp.sum(qre * dmix, axis=-1, keepdims=True)
        yield
        moved = dot(pb, dy, 0, 0).astype(DX)
        yield
        dx = dot(mb, moved, 0, 0)
        yield
        dx_ref[i] = dx
        left = jnp.concatenate([qb, kb], 0)
        right = jnp.concatenate(
            [(eg * dmix).astype(OUTER), (-(eg * beta) * dx).astype(OUTER)], 0
        )
        local_ref[pl.ds(i * size, size), :] = dot(left, right, 0, 0).astype(BF)

    interleave(one(i) for i in range(half))
    total = sum(totals[1:], totals[0])
    if len(refs) > 9:
        total = total + refs[0][...]
    total_ref[...] = total
    local_ref[half * size : half * size + 16, :] = gain_rows(total)


def query_kernel(heads, base_ref, q_ref, g_ref, *refs):
    half = heads // 2
    dgc_ref, dgr_ref, dq_ref = refs[-3:]
    base = (base_ref[0] & 1) * (heads // 2)
    rows = dq_ref.shape[0]
    size = refs[0].shape[2]
    row, col = ids(rows, rows)
    within = row >= col
    g_all = g_ref[...]
    g_rows = g_all.T
    dgc_ref[...] = refs[7][...] + refs[15][...]
    dgr_ref[...] = jnp.zeros_like(dgr_ref)

    def one(s):
        i, side = s % half, s // half
        state_ref, kb_ref, qb_ref, m_ref, p_ref, u_ref, dy_ref, _ = refs[8 * side : 8 * side + 8]
        dkp_ref, mk_ref = refs[16 + 2 * side : 18 + 2 * side]
        cols = head_cols(base, s, size)
        kb, qb, dy, pb = kb_ref[i], qb_ref[i], dy_ref[i], p_ref[i]
        gc = g_all[:, s : s + 1]
        end = g_rows[s : s + 1, rows - 1 : rows]
        fade = jnp.exp(jnp.where(within, gc - g_rows[s : s + 1, :], 0.0))
        dp = dot(dy, u_ref[i], 1, 1)
        yield
        dpf = jnp.where(within, dp * fade, 0.0).astype(BF)
        moved = dp * pb.astype(F32)
        dgc_ref[:, s : s + 1] += jnp.sum(moved, axis=1, keepdims=True)
        dgr_ref[s : s + 1, :] = -jnp.sum(moved, axis=0, keepdims=True)
        left = jnp.concatenate([(jnp.exp(gc) * dy.astype(F32)).astype(BF), dpf], 1)
        right = jnp.concatenate([state_ref[i].T, kb.astype(BF)], 0)
        dunit = dot(left, right)
        yield
        unit, inv = unit_of(q_ref[:, cols].astype(F32))
        dq_ref[:, cols] = (
            (inv * size**-0.5) * (dunit - unit * jnp.sum(unit * dunit, axis=-1, keepdims=True))
        ).astype(BF)
        dkp_ref[i] = dot(dpf, qb.astype(BF), 0, 0)
        tail = (jnp.exp(end - gc) * kb.astype(F32)).astype(MK)
        mk_ref[i] = dot(m_ref[i], tail, 0, 0).astype(MK)
        yield

    interleave(one(s) for s in range(heads))


def decay_kernel(
    heads, first, final, base_ref, state_ref, grad_ref, k_ref, v_ref, n_ref, g_ref, b_ref, u_ref, kre_ref,
    dx_ref, mk_ref, dgc_in, dgr_in, *refs,
):
    if not final:
        dmat_ref, dtail_ref, gdv_ref, dgc, dgr, dbc, dv_ref = refs
        dgc[...] = dgc_in[...]
        dgr[...] = dgr_in[...]
        dbc[...] = jnp.zeros_like(dbc)
    else:
        (
            decay_ref, log_ref, dbc_far, gain_ref, _, dmat_ref, dtail_ref, gdv_ref, dbeta_ref,
            ddecay_ref, small_ref, dv_ref, dgc, dgr, dbc, pad,
        ) = refs
        dgc[...] = dgc_in[...]
        dgr[...] = dgr_in[...]
        dbc[...] = dbc_far[...]
    base = (base_ref[0] & 1) * (heads // 2)
    rows = dv_ref.shape[0]
    size = mk_ref.shape[2]
    lanes = g_ref.shape[1]
    row, col = ids(rows, rows)
    within = row >= col
    strict = row > col
    last = lax.broadcasted_iota(jnp.int32, (rows, 1), 0) == rows - 1
    g_all = g_ref[...]
    g_rows = g_all.T

    def one(i):
        s = first + i
        cols = head_cols(base, s, size)
        update = u_ref[i]
        gc = g_all[:, s : s + 1]
        beta = b_ref[:, s : s + 1]
        end = g_rows[s : s + 1, rows - 1 : rows]
        state, grad = state_ref[i], grad_ref[i]
        fade = jnp.exp(jnp.where(within, gc - g_rows[s : s + 1, :], 0.0))
        dx = dx_ref[i] + dot(mk_ref[i], grad)
        yield
        kre = kre_ref[i].astype(F32)
        dv = beta * dx
        dv_ref[:, fixed_cols(i, size)] = dv.astype(BF)
        gdv_ref[i] = (-jnp.exp(gc) * dv).astype(BF)
        da = jnp.where(strict, -dot(dx.astype(GDX), update, 1, 1), 0.0)
        yield
        by_beta = da * n_ref[i].astype(F32)
        moved = beta * by_beta
        dbc[:, s : s + 1] = jnp.sum(
            by_beta + dx * (v_ref[:, cols].astype(F32) - kre), axis=1, keepdims=True
        )
        dmat_ref[i] = (da * (beta * fade)).astype(BF)
        dtail = jnp.exp(end - gc) * dot(update, grad, 1, 1)
        yield
        dtail_ref[i] = dtail
        unit = unit_of(k_ref[:, cols].astype(F32))[0]
        ends = dtail * unit
        dend = jnp.sum(
            jnp.sum(ends, axis=0, keepdims=True)
            + jnp.exp(end)
            * jnp.sum(state.astype(F32) * grad.astype(F32), axis=0, keepdims=True),
            axis=1,
            keepdims=True,
        )
        dgc[:, s : s + 1] = (
            dgc[:, s : s + 1]
            + jnp.sum(moved - ends - kre * dv, axis=1, keepdims=True)
            + jnp.where(last, dend, 0.0)
        )
        dgr[s : s + 1, :] = dgr[s : s + 1, :] - jnp.sum(moved, axis=0, keepdims=True)

    interleave(one(i) for i in range(heads // 2))
    if not final:
        return
    perm = slot_matrix(base, heads, lanes)
    ahead = jnp.where(row <= col, 1.0, 0.0).astype(F32)
    ddecay = dot(
        perm, dot(ahead, dgc[...] + dgr[...].T, precision=HIGHEST), 1, 1, precision=HIGHEST
    )[:heads]
    betas = b_ref[...]
    dbeta = dot(perm, dbc[...] * betas * (1.0 - betas), 1, 1, precision=HIGHEST)
    dbeta_ref[...] = dbeta[:heads]
    rate = rate_of(log_ref, heads)
    inputs = decay_ref[...]
    ddecay_ref[...] = ddecay * rate * sigmoid(inputs)
    pad[...] = jnp.zeros_like(pad)
    pad[:heads, :] = ddecay * rate * softplus(inputs)
    small_ref[0:1, :] = jnp.sum(pad[...].T, axis=0, keepdims=True)
    small_ref[1:2, :] = gain_ref[...]


def key_kernel(heads, base_ref, k_ref, *refs):
    half = heads // 2
    dk_ref = refs[-1]
    base = (base_ref[0] & 1) * (heads // 2)
    size = refs[0].shape[2]

    def one(s):
        i, side = s % half, s // half
        state_ref, kb_ref, dkp_ref, gdv_ref, dmat_ref, dtail_ref = refs[6 * side : 6 * side + 6]
        cols = head_cols(base, s, size)
        dmat = dmat_ref[i].astype(F32)
        left = jnp.concatenate([(dmat + dmat.T).astype(BF), gdv_ref[i]], 1)
        right = jnp.concatenate([kb_ref[i].astype(BF), state_ref[i].T], 0)
        yield
        dunit = dkp_ref[i] + dot(left, right) + dtail_ref[i]
        yield
        unit, inv = unit_of(k_ref[:, cols].astype(F32))
        dk_ref[:, cols] = (
            inv * (dunit - unit * jnp.sum(unit * dunit, axis=-1, keepdims=True))
        ).astype(BF)

    interleave(one(s) for s in range(heads))


def pair_kernel(_, first_ref, second_ref, out_ref, sems):
    cut = first_ref.shape[1]
    fetch_all((first_ref, second_ref), (out_ref.at[0, :, :cut], out_ref.at[0, :, cut:]), sems)


def join_kernel(_, first_ref, second_ref, out_ref):
    cut = first_ref.shape[0]
    out_ref[:cut] = first_ref[...]
    out_ref[cut:] = second_ref[...]


def end_kernel(_, sums_ref, moved_ref, *refs):
    log_ref, gain_ref = refs[-2:]
    count = log_ref.shape[1]
    log_ref[...] = sums_ref[0:1, :count] + moved_ref[0:1, :count]
    gain = sums_ref[1:2, :]
    for ref in refs[:-2]:
        gain = gain + ref[1:2, :]
    gain_ref[...] = gain


def half_sum_kernel(parts, _, own_ref, moved_ref, keep_ref, send_ref):
    keep_ref[...] = own_ref[:parts] + moved_ref[:parts].astype(F32)
    send_ref[...] = (own_ref[parts:] + moved_ref[parts:].astype(F32)).astype(BF)


def last_sum_kernel(_, own_ref, moved_ref, key_ref, value_ref):
    total = own_ref[0] + moved_ref[0].astype(F32)
    cut = key_ref.shape[1]
    key_ref[...] = total[:, :cut].astype(BF)
    value_ref[...] = total[:, cut:].astype(BF)


def attention_kernel(offsets, start, end, here_ref, q_ref, gate_ref, cot_ref, near_ref, far_ref, *refs):
    raised_ref, weights_ref, score_ref = refs[-3:]
    if start:
        ins, outs = (), refs[:-3]
    else:
        ins, outs = refs[:3], refs[6:-3]
    out_ref, dq_ref, dgate_ref = outs[:3]
    count = len(offsets)
    half = count // 2
    here = here_ref[0]
    rows = q_ref.shape[0]
    size = near_ref.shape[2] // 2
    group = q_ref.shape[1] // size
    wide = group * rows
    scaling = size**-0.5

    def keys_of(k):
        return (near_ref if k < half else far_ref)[k % half][:, :size]

    def values_of(k):
        return (near_ref if k < half else far_ref)[k % half][:, size:]

    if start:
        keys_t, values_t = outs[3:5]
        for k in range(count):
            part = pl.ds(k * rows, rows)
            keys_t[:, part] = keys_of(k).T
            values_t[:, part] = values_of(k).T
    else:
        keys_t, values_t, total_in = ins

    def stack(ref):
        return jnp.concatenate([ref[:, i * size : (i + 1) * size] for i in range(group)], 0)

    def spread(ref, value):
        for i in range(group):
            ref[:, i * size : (i + 1) * size] = value[i * rows : (i + 1) * rows].astype(ref.dtype)

    queries = (stack(q_ref).astype(F32) * scaling).astype(BF)
    key_at, query_at = ids(rows, wide)
    own = key_at <= (query_at % rows)
    top = jnp.full((1, wide), NEG_FILL, F32)
    biases = [jnp.where((here ^ x) < here, 0.0, NEG_FILL) if x else 0.0 for x in offsets]
    for k in range(count):
        scores = dot(keys_of(k), queries, 1, 1)
        if offsets[k] == 0:
            scores = jnp.where(own, scores, NEG_FILL)
        raised_ref[pl.ds(k * rows, rows), :] = scores
        top = jnp.maximum(top, jnp.max(scores, axis=0, keepdims=True) + biases[k])
    total = jnp.zeros((1, wide), F32)
    for k in range(count):
        part = pl.ds(k * rows, rows)
        raised = jnp.exp(raised_ref[part, :] - (top - biases[k]))
        raised_ref[part, :] = raised
        total = total + jnp.sum(raised, axis=0, keepdims=True)
    scale = 1.0 / total
    for k in range(count):
        part = pl.ds(k * rows, rows)
        weights_ref[part, :] = (raised_ref[part, :] * scale).astype(BF)
    attended_t = dot(values_t[...], weights_ref[...])
    attended = attended_t.T
    gate = stack(gate_ref).astype(F32)
    cot = stack(cot_ref).astype(F32)
    opening = sigmoid(gate)
    spread(out_ref, attended * opening)
    up = (cot * opening).astype(BF)
    spread(dgate_ref, cot * attended * opening * (1.0 - opening))
    up_t = up.T
    centering = jnp.sum(up_t.astype(F32) * attended_t, axis=0, keepdims=True) * scale
    for k in range(count):
        part = pl.ds(k * rows, rows)
        weight_grad = dot(values_of(k), up_t)
        score_ref[part, :] = (raised_ref[part, :] * (weight_grad * scale - centering)).astype(BF)
    dq_t = dot(keys_t[...], score_ref[...]) * scaling
    spread(dq_ref, dq_t.T)
    dk = dot(score_ref[...], queries)
    dv = dot(weights_ref[...], up)
    for k in range(count):
        part = slice(k * rows, (k + 1) * rows)
        if end:
            target, at = (outs[3] if k < half else outs[4]), k % half
        else:
            target, at = outs[-1], k
        dk_part, dv_part = dk[part], dv[part]
        if not start:
            dk_part = dk_part + total_in[k, :, :size]
            dv_part = dv_part + total_in[k, :, size:]
        target[at, :, :size] = dk_part.astype(target.dtype)
        target[at, :, size:] = dv_part.astype(target.dtype)


def call(kernel, outs, scratch, base, *args, blocked=(), prior=None, side=0, far=False):
    vmem = pl.BlockSpec(memory_space=pltpu.VMEM)
    hbm = pl.BlockSpec(memory_space=pl.ANY)
    if far:
        args = tuple(pltpu.with_memory_space_constraint(x, pltpu.HBM) for x in args)
    args = tuple(args) + tuple(prior or ())
    count = len(args) + 1 - len(prior or ())
    return pl.pallas_call(
        kernel,
        out_shape=tuple(jax.ShapeDtypeStruct(shape, dtype) for shape, dtype in tuple(outs) + tuple(blocked)),
        grid_spec=pltpu.PrefetchScalarGridSpec(
            num_scalar_prefetch=1,
            grid=(1,),
            in_specs=[pl.BlockSpec(memory_space=pltpu.HBM) if far else vmem] * (count - 1) + [hbm] * len(prior or ()),
            out_specs=tuple(vmem for _ in outs)
            + tuple(
                pl.BlockSpec((shape[0], shape[1] // 2), lambda i, where: (0, (where[0] & 1) ^ side))
                for shape, _ in blocked
            ),
            scratch_shapes=scratch,
        ),
        input_output_aliases={count + i: len(outs) + i for i in range(len(prior or ()))},
        compiler_params=pltpu.CompilerParams(vmem_limit_bytes=VMEM_LIMIT),
    )(base, *args)


def swap(value, axis, offset):
    count = lax.axis_size(axis)
    return lax.ppermute(value, axis, [(i, i ^ offset) for i in range(count)])


def axis_sum(value, axis):
    offset = 1
    while offset < lax.axis_size(axis):
        value = value + swap(value, axis, offset)
        offset *= 2
    return value


def per_device(
    delta_query,
    delta_key,
    delta_value,
    beta_logit,
    decay_input,
    decay_log,
    norm_gain,
    output_gate,
    delta_cotangent,
    attn_query,
    attn_key,
    attn_value,
    attn_gate,
    attn_cotangent,
):
    tokens = delta_query.shape[1]
    heads = decay_log.shape[0]
    size = norm_gain.shape[0]
    lanes = 128
    count = lax.axis_size("ctx")
    levels = count.bit_length() - 1
    here = lax.axis_index("ctx").astype(jnp.int32)
    half = heads // 2
    spot = here.reshape(1)

    rows_att, key_width = attn_key.shape[1], attn_key.shape[2]
    (near_kv,) = call(
        pair_kernel, [((1, rows_att, 2 * key_width), BF)], [pltpu.SemaphoreType.DMA((2,))],
        spot, attn_key[0], attn_value[0], far=True,
    )
    offsets = [0]
    jump = count // 2
    while jump > 1:
        moved = swap(near_kv, "ctx", jump)
        (near_kv,) = call(
            join_kernel,
            [((2 * near_kv.shape[0],) + near_kv.shape[1:], BF)], [], spot, near_kv, moved,
        )
        offsets += [x ^ jump for x in offsets]
        jump //= 2
    far_kv = swap(near_kv, "ctx", 1)
    offsets += [x ^ 1 for x in offsets]

    q, k, v = delta_query[0], delta_key[0], delta_value[0]
    beta, decay, logs = beta_logit[0].T, decay_input[0].T, decay_log[None]
    column = ((tokens, lanes), F32)
    turned = ((lanes, tokens), F32)
    flat = ((tokens, heads * size), BF)
    small = ((heads, tokens), F32)
    maps = ((half, size, 2 * size), BF)
    states = ((half, size, size), BF)
    cube = ((half, tokens, size), BF)
    cube_wide = ((half, tokens, size), F32)
    square = ((half, tokens, tokens), BF)
    packed = ((half * size + 16, size), BF)
    column_scratch = pltpu.VMEM(*column)

    kept = [maps, (cube[0], KQ), (square[0], INV), (square[0], SCO)]
    results = call(
        functools.partial(prepare_kernel, heads), kept + kept + [column, column],
        [pltpu.VMEM(*turned)]
        + [pltpu.VMEM(x.shape, x.dtype) for x in (k, v, beta, decay, logs)]
        + [pltpu.SemaphoreType.DMA((5,))],
        spot, k, v, beta, decay, logs, far=True,
    )
    keep, kb_near, m_near, n_near = results[:4]
    send, kb_far, m_far, n_far = results[4:8]
    g, b = results[8:]
    qb_near, p_near, qb_far, p_far = call(
        functools.partial(score_kernel, heads), [(cube[0], KQ), (square[0], SCO)] * 2, [],
        spot, q, g, kb_near, kb_far,
    )
    near = [kb_near, qb_near, m_near, p_near, n_near]
    far = [kb_far, qb_far, m_far, p_far, n_far]
    pairs = []
    for level in range(levels - 1):
        moved = swap(send, "ctx", 1 << level)
        pair, total = call(
            functools.partial(up_kernel, level),
            [((2,) + maps[0], BF), maps if level < levels - 2 else states],
            [], spot, keep, moved,
        )
        pairs.append(pair)
        keep = send = total
    moved = swap(send, "ctx", 1 << (levels - 1))
    near_state, send = call(
        functools.partial(down_kernel, levels), [states, states], [], spot, moved, *pairs
    )
    far_state = swap(send, "ctx", 1)
    gain = norm_gain[None]
    gates = output_gate[0], delta_cotangent[0], gain
    kept = [packed, (cube[0], UPD), (cube[0], KRE), (cube[0], DY), cube_wide, column, ((1, size), F32)]
    keep, *near_out, dg_near, gain_near, out, dgate = call(
        functools.partial(output_kernel, heads, 0), kept, [],
        spot, near_state, v, *gates, near[0], near[1], near[2], near[3], g, b,
        blocked=[flat, flat],
    )
    send, *far_out, dg_far, _, out, dgate = call(
        functools.partial(output_kernel, heads, half), kept, [],
        spot, far_state, v, *gates, far[0], far[1], far[2], far[3], g, b, gain_near,
        blocked=[flat, flat], prior=[out, dgate], side=1,
    )
    locals_ = []
    for level in range(levels - 1):
        moved = swap(send, "ctx", 1 << level)
        both, total = call(
            functools.partial(up_back_kernel, level, half),
            [((2,) + packed[0], BF), packed],
            [], spot, pairs[level], keep, moved, send,
        )
        locals_.append(both)
        keep = send = total
    moved = swap(send, "ctx", 1 << (levels - 1))
    near_grad, send, gain_part = call(
        functools.partial(down_back_kernel, levels, half), [states, states, ((1, size), F32)], [],
        spot, keep, moved, *pairs, *locals_,
    )
    far_grad = swap(send, "ctx", 1)
    dkp_near, mk_near, dkp_far, mk_far, dgc, dgr, dq = call(
        functools.partial(query_kernel, heads),
        [cube_wide, (cube[0], MK), cube_wide, (cube[0], MK), column, turned, flat], [], spot, q, g,
        near_state, near[0], near[1], near[2], near[3], near_out[0], near_out[2], dg_near,
        far_state, far[0], far[1], far[2], far[3], far_out[0], far_out[2], dg_far,
    )
    dmat_near, dtail_near, gdv_near, dgc, dgr, dbc, dv = call(
        functools.partial(decay_kernel, heads, 0, False),
        [square, cube_wide, cube, column, turned, column], [],
        spot, near_state, near_grad, k, v, near[4], g, b, near_out[0], near_out[1], near_out[3],
        mk_near, dgc, dgr,
        blocked=[flat],
    )
    dmat_far, dtail_far, gdv_far, dbeta, ddecay, sums, dv = call(
        functools.partial(decay_kernel, heads, half, True),
        [square, cube_wide, cube, small, small, ((2, lanes), F32)],
        [column_scratch, pltpu.VMEM(*turned), column_scratch, column_scratch],
        spot, far_state, far_grad, k, v, far[4], g, b, far_out[0], far_out[1], far_out[3],
        mk_far, dgc, dgr, decay, logs, dbc, gain_part,
        blocked=[flat], prior=[dv], side=1,
    )
    (dk,) = call(
        functools.partial(key_kernel, heads), [flat], [], spot, k,
        near_state, near[0], dkp_near, gdv_near, dmat_near, dtail_near,
        far_state, far[0], dkp_far, gdv_far, dmat_far, dtail_far,
    )
    sums = axis_sum(sums, "section")
    offset, partner = 1, []
    while offset < lax.axis_size("head"):
        partner.append(swap(sums, "head", offset))
        offset *= 2
    summed = lax.broadcasted_iota(jnp.int32, sums.shape, 0) == 0
    for level in range(levels - 1):
        moved = swap(sums, "ctx", 1 << level)
        sums = sums + jnp.where(summed, moved, 0.0)
    moved = swap(sums, "ctx", 1 << (levels - 1))
    log_grad, gain_grad = call(
        end_kernel, [((1, heads), F32), ((1, size), F32)], [], spot, sums, moved, *partner
    )

    groups = attn_query.shape[2] // AD
    group = 2 if groups % 2 == 0 else 1
    calls = groups // group
    length = count * rows_att
    vmem = pl.BlockSpec(memory_space=pltpu.VMEM)
    wide = jax.ShapeDtypeStruct((rows_att, groups * AD), BF)
    turned_kv = jax.ShapeDtypeStruct((AD, length), BF)
    terms = jax.ShapeDtypeStruct((count, rows_att, 2 * key_width), F32)
    extra, outs = [], []
    for j in range(calls):
        start, end = j == 0, j == calls - 1
        block = pl.BlockSpec((rows_att, group * AD), lambda i, where, j=j: (0, j))
        tail = [turned_kv, turned_kv] if start else []
        if end:
            tail = tail + [
                jax.ShapeDtypeStruct(near_kv.shape, F32), jax.ShapeDtypeStruct(near_kv.shape, BF)
            ]
        else:
            tail = tail + [terms]
        results = pl.pallas_call(
            functools.partial(attention_kernel, offsets, start, end),
            grid_spec=pltpu.PrefetchScalarGridSpec(
                num_scalar_prefetch=1,
                grid=(1,),
                in_specs=[block, block, block] + [vmem] * (2 + len(extra))
                + [pl.BlockSpec(memory_space=pl.ANY)] * len(outs),
                out_specs=[block, block, block] + [vmem] * len(tail),
                scratch_shapes=[
                    pltpu.VMEM((length, group * rows_att), dtype) for dtype in (F32, BF, BF)
                ],
            ),
            out_shape=[wide, wide, wide] + tail,
            input_output_aliases={6 + len(extra) + i: i for i in range(len(outs))},
            compiler_params=pltpu.CompilerParams(vmem_limit_bytes=VMEM_LIMIT),
        )(spot, attn_query[0], attn_gate[0], attn_cotangent[0], near_kv, far_kv, *extra, *outs)
        outs = results[:3]
        if start:
            keys_t, values_t = results[3:5]
        extra = [keys_t, values_t, results[-1]]
    attn_out, dquery, dgate_att = outs
    own, send = results[-2:]
    jump = 1
    while jump < count:
        moved = swap(send, "ctx", jump)
        parts = own.shape[0] // 2
        if parts:
            own, send = call(
                functools.partial(half_sum_kernel, parts),
                [((parts,) + own.shape[1:], F32), ((parts,) + own.shape[1:], BF)], [],
                spot, own, moved,
            )
        else:
            dkey, dvalue = call(
                last_sum_kernel, [((rows_att, key_width), BF)] * 2, [], spot, own, moved
            )
        jump *= 2
    return (
        out[None],
        dq[None],
        dk[None],
        dv[None],
        dbeta.T[None],
        ddecay.T[None],
        log_grad[0],
        gain_grad[0],
        dgate[None],
        attn_out[None],
        dquery[None],
        dkey[None],
        dvalue[None],
        dgate_att[None],
    )


def solution(mesh):
    split = P("section", "ctx", "head")
    in_specs = (split,) * 5 + (P("head"), P()) + (split,) * 7
    out_specs = (split,) * 6 + (P("head"), P()) + (split,) * 6

    return jax.shard_map(
        per_device, mesh=mesh, in_specs=in_specs, out_specs=out_specs, check_vma=False
    )
```
